128 devices in a mesh: rep: 8 (over x_hi, y), gx: 4 (over x_lo, core), gy: 4 (over z).
Axes of the slice: x: 4 (x_hi: 2, x_lo: 2; x = x_hi * 2 + x_lo), y: 4, z: 4, core: 2. Of those that a mesh axis runs over, the one named last changes fastest.
Arguments:
- deltas: bfloat16 [8, 2, 3584, 14336], P('rep', None, 'gx', 'gy'), may hold values from -32 to 32
- params: float32 [2, 4, 4, 8, 4, 4, 28, 896], P(None, None, 'gx', 'rep', None, 'gy'), may hold values from -0.75 to 0.75
- momentum: float32 [2, 4, 4, 8, 4, 4, 28, 896], P(None, None, 'gx', 'rep', None, 'gy'), may hold values from -1.5 to 1.5
Outputs:
- new_params: float32 [2, 4, 4, 8, 4, 4, 28, 896], P(None, None, 'gx', 'rep', None, 'gy')
- new_momentum: float32 [2, 4, 4, 8, 4, 4, 28, 896], P(None, None, 'gx', 'rep', None, 'gy')
The draws below stay inside these ranges and needn't reach their ends.
All inputs are finite; a program needn't handle non-finite values.
Results may differ from the reference program's by a relative error of at most 0.0003.
Values may be sent and summed in bfloat16 or wider, within the bound.
No kernel may reach another device: no remote copies, remote signals or barrier semaphores. Data moves between devices by JAX's collectives and lax.ppermute only.
A program may use at most 128 MiB of HBM per device.

```python
import math
import jax
import jax.numpy as jnp
from jax import lax

D = 3584
FF = 14336
REPLICAS = 8
ROW_SPLIT = 4
COL_SPLIT = 4
ROW_TILE = 28
COL_TILE = 896


def draw_deltas(key, part):
    row_key, col_key, own_key = jax.random.split(key, 3)
    devices_all = REPLICAS * ROW_SPLIT * COL_SPLIT
    divisor = 2.0 * max(devices_all - 1, 1)
    rows_at = jnp.arange(D) % (D // ROW_SPLIT) // ROW_TILE
    rep_at = rows_at % REPLICAS
    gx_at = rows_at // REPLICAS
    cols_at = jnp.arange(FF) % (FF // COL_SPLIT) // COL_TILE
    row_ramp = jnp.exp(math.log(3.0) * (rep_at * ROW_SPLIT * COL_SPLIT + gx_at * COL_SPLIT).astype(jnp.float32) / divisor)
    col_ramp = jnp.exp(math.log(3.0) * cols_at.astype(jnp.float32) / divisor)
    row_scale = jnp.power(10.0, jax.random.uniform(row_key, (2, D, 1), jnp.float32)) * row_ramp[None, :, None]
    col_scale = jnp.power(10.0, jax.random.uniform(col_key, (2, 1, FF), jnp.float32)) * col_ramp[None, None, :]
    spread = 0.1 * row_scale * col_scale

    def draw_replica(replica):
        sample = jax.random.truncated_normal(jax.random.fold_in(own_key, replica), -6.0, 6.0, (2, D, FF), jnp.float32)
        value = jnp.clip(sample * spread, -32.0, 32.0)
        return value.astype(jnp.bfloat16)
    return lax.map(draw_replica, jnp.arange(REPLICAS))


def shard_levels(key, extent, pieces, low, top_value):
    def one(position, blocks):
        heights = jax.random.uniform(jax.random.fold_in(jax.random.fold_in(key, 6), position), (blocks,), jnp.float32, low / len(pieces), top_value / len(pieces))
        return jnp.repeat(jnp.exp(heights), extent[position] // blocks).reshape((-1,) + (1,) * (len(extent) - position - 1))

    loudness = one(*pieces[0])
    for cut in pieces[1:]:
        loudness = loudness * one(*cut)
    return loudness


def bell_draw(key, shape, width, reach, shards=(), kind=jnp.bfloat16):
    values = jax.random.normal(key, shape, jnp.float32) * width
    if len(shards) > 0:
        values = shard_levels(key, shape, shards, -0.22, 0.18) * values
    return jnp.clip(values, min=-reach, max=reach).astype(kind)


def setup_inputs(seed: int = 0) -> dict:
    seeds = jax.random.split(jax.random.key(seed), 4)
    return {
        "deltas": draw_deltas(jax.random.fold_in(seeds[3], 71), 0),
        "params": bell_draw(seeds[1], (2, ROW_SPLIT, ROW_SPLIT, REPLICAS, COL_SPLIT, COL_SPLIT, ROW_TILE, COL_TILE), 0.05, 0.75, ((2, 4), (3, 8), (5, 4)), jnp.float32),
        "momentum": bell_draw(seeds[2], (2, ROW_SPLIT, ROW_SPLIT, REPLICAS, COL_SPLIT, COL_SPLIT, ROW_TILE, COL_TILE), 0.1, 1.5, ((2, 4), (3, 8), (5, 4)), jnp.float32),
    }


clip_level = 0.25
moment_decay = 0.9
outer_rate = 0.7
epsilon = 1e-06

def reference(deltas, params, momentum):
    running = jnp.zeros(deltas.shape[1:], jnp.float32)
    for replica in range(REPLICAS):
        running = running + deltas[replica].astype(jnp.float32)
    mean_delta = running / REPLICAS
    squares = jnp.sum(mean_delta * mean_delta)
    entries = mean_delta.size
    root_mean = jnp.sqrt(squares / entries + epsilon)
    clip_scale = jnp.minimum(1.0, clip_level / root_mean)
    blocked = mean_delta.reshape(2, ROW_SPLIT, ROW_SPLIT, REPLICAS, ROW_TILE, COL_SPLIT, COL_SPLIT, COL_TILE)
    blocked = jnp.transpose(blocked, (0, 1, 2, 3, 5, 6, 4, 7))
    gradient = clip_scale * blocked
    new_momentum = moment_decay * momentum + gradient
    new_params = params - outer_rate * (gradient + moment_decay * new_momentum)
    return (new_params, new_momentum)
```

```python
import jax
import jax.numpy as jnp
from jax import lax
from jax.experimental import pallas as pl
from jax.experimental.pallas import tpu as pltpu
from jax.sharding import Mesh
from jax.sharding import PartitionSpec as P

GX = ("gx_0", "gx_1")
REP = ("rep_0", "rep_1")
EVERY = ("rep_0", "rep_1", "gx_0", "gx_1", "gy")
LANES = 128

clip_level = 0.25
moment_decay = 0.9
outer_rate = 0.7
epsilon = 1e-06


def pack_kernel(replicas, row_tile, x_ref, out_ref):
    for r in range(replicas):
        for m in range(2):
            out_ref[r, 0, 0, m * row_tile : (m + 1) * row_tile, :] = x_ref[
                m, r * row_tile : (r + 1) * row_tile, :
            ]


def pack(deltas, replicas, rows_split, cols_split, row_tile, col_tile):
    block_rows = replicas * row_tile
    return pl.pallas_call(
        lambda x_ref, out_ref: pack_kernel(replicas, row_tile, x_ref, out_ref),
        name="pack",
        grid=(rows_split, cols_split),
        in_specs=[pl.BlockSpec((2, block_rows, col_tile), lambda c, d: (0, c, d))],
        out_specs=pl.BlockSpec(
            (replicas, 1, 1, 2 * row_tile, col_tile), lambda c, d: (0, c, d, 0, 0)
        ),
        out_shape=jax.ShapeDtypeStruct(
            (replicas, rows_split, cols_split, 2 * row_tile, col_tile), deltas.dtype
        ),
        compiler_params=pltpu.CompilerParams(vmem_limit_bytes=24 << 20),
    )(deltas)


def mean_kernel(replicas, blocks, row_tile, col_tile, x_ref, mean_ref, squares_ref):
    lane_tiles = col_tile // LANES
    squares_ref[...] = jnp.zeros_like(squares_ref)

    def block(ab, carry):
        for group in range(2 * row_tile // 8):
            total = x_ref[0, ab, group * 8 : group * 8 + 8, :].astype(jnp.float32)
            for replica in range(1, replicas):
                total = total + x_ref[
                    replica, ab, group * 8 : group * 8 + 8, :
                ].astype(jnp.float32)
            mean = total * (1.0 / replicas)
            square = mean * mean
            partial = square[:, :LANES]
            for j in range(1, lane_tiles):
                partial = partial + square[:, j * LANES : (j + 1) * LANES]
            squares_ref[...] += partial
            row = 0
            while row < 8:
                at = group * 8 + row
                m, i = at // row_tile, at % row_tile
                count = min(8 - row, row_tile - i)
                start = ((m * blocks + ab) * row_tile + i) * lane_tiles
                for j in range(lane_tiles):
                    mean_ref[pl.ds(start + j, count, stride=lane_tiles), :] = mean[
                        row : row + count, j * LANES : (j + 1) * LANES
                    ]
                row += count
        return carry

    lax.fori_loop(0, blocks, block, 0)


def average(received, row_tile, col_tile):
    replicas, blocks = received.shape[:2]
    size = blocks * 2 * row_tile * col_tile
    return pl.pallas_call(
        lambda *refs: mean_kernel(replicas, blocks, row_tile, col_tile, *refs),
        name="average",
        in_specs=[pl.BlockSpec(memory_space=pltpu.VMEM)],
        out_specs=[pl.BlockSpec(memory_space=pltpu.VMEM)] * 2,
        out_shape=[
            jax.ShapeDtypeStruct((size // LANES, LANES), jnp.float32),
            jax.ShapeDtypeStruct((8, LANES), jnp.float32),
        ],
        compiler_params=pltpu.CompilerParams(vmem_limit_bytes=24 << 20),
    )(received)


def step_kernel(entries, squares_ref, mean_ref, params_ref, momentum_ref, params_out, momentum_out):
    squares = jnp.sum(squares_ref[...], keepdims=True)
    root_mean = jnp.sqrt(squares * (1.0 / entries) + epsilon)
    clip_scale = jnp.minimum(1.0, clip_level / root_mean)
    gradient = clip_scale * mean_ref[...]
    momentum = moment_decay * momentum_ref[...] + gradient
    momentum_out[...] = momentum
    params_out[...] = params_ref[...] - outer_rate * (gradient + moment_decay * momentum)


def step(squares, mean, params, momentum, entries):
    rows = mean.shape[0]
    pieces = 8
    whole = pl.BlockSpec(squares.shape, lambda i: (0, 0))
    tile = pl.BlockSpec((rows // pieces, LANES), lambda i: (i, 0))
    return pl.pallas_call(
        lambda *refs: step_kernel(entries, *refs),
        name="outer_step",
        grid=(pieces,),
        in_specs=[whole, tile, tile, tile],
        out_specs=[tile, tile],
        out_shape=[jax.ShapeDtypeStruct(mean.shape, jnp.float32)] * 2,
        compiler_params=pltpu.CompilerParams(vmem_limit_bytes=16 << 20),
    )(squares, mean, params, momentum)


def per_device(deltas, params, momentum):
    rows_split = lax.axis_size(GX)
    cols_split = lax.axis_size("gy")
    replicas = lax.axis_size(REP)
    devices = rows_split * cols_split * replicas
    matrices, local_rows, local_cols = deltas.shape[1:]
    row_tile = local_rows // (rows_split * replicas)
    col_tile = local_cols // cols_split
    entries = matrices * local_rows * local_cols * rows_split * cols_split
    packed = pack(deltas[0], replicas, rows_split, cols_split, row_tile, col_tile)
    packed = packed.reshape(devices, 2 * row_tile, col_tile)
    received = lax.all_to_all(packed, EVERY, split_axis=0, concat_axis=0, tiled=True)
    received = received.reshape(replicas, rows_split * cols_split, 2 * row_tile, col_tile)
    mean, squares = average(received, row_tile, col_tile)
    squares = jnp.sum(squares, axis=0, keepdims=True)
    squares = jnp.broadcast_to(squares[None], (devices, 1, LANES))
    squares = lax.all_to_all(squares, EVERY, split_axis=0, concat_axis=0, tiled=True)
    flat = mean.shape
    new_params, new_momentum = step(
        squares.reshape(devices, LANES), mean, params.reshape(flat), momentum.reshape(flat), entries
    )
    return new_params.reshape(params.shape), new_momentum.reshape(params.shape)


def solution(mesh):
    finer = Mesh(
        mesh.devices.reshape(2, 4, 2, 2, mesh.shape["gy"]), ("rep_0", "rep_1", "gx_0", "gx_1", "gy")
    )
    return jax.shard_map(
        per_device,
        mesh=finer,
        in_specs=(
            P(REP, None, GX, "gy"),
            P(None, None, GX, REP, None, "gy", None, None),
            P(None, None, GX, REP, None, "gy", None, None),
        ),
        out_specs=(
            P(None, None, GX, REP, None, "gy", None, None),
            P(None, None, GX, REP, None, "gy", None, None),
        ),
        check_vma=False,
    )
```

```python
import jax
import jax.numpy as jnp
from jax import lax
from jax.experimental import pallas as pl
from jax.experimental.pallas import tpu as pltpu
from jax.sharding import Mesh
from jax.sharding import PartitionSpec as P

GX = ("gx_0", "gx_1")
REP = ("rep_0", "rep_1")
EVERY = ("rep_0", "rep_1", "gx_0", "gx_1", "gy")
LANES = 128

clip_level = 0.25
moment_decay = 0.9
outer_rate = 0.7
epsilon = 1e-06


def pack_kernel(replicas, row_tile, x_ref, out_ref):
    for r in range(replicas):
        for m in range(2):
            out_ref[r, 0, 0, m * row_tile : (m + 1) * row_tile, :] = x_ref[
                m, r * row_tile : (r + 1) * row_tile, :
            ]


def pack(deltas, replicas, rows_split, cols_split, row_tile, col_tile):
    block_rows = replicas * row_tile
    return pl.pallas_call(
        lambda x_ref, out_ref: pack_kernel(replicas, row_tile, x_ref, out_ref),
        name="pack",
        grid=(rows_split, cols_split),
        in_specs=[pl.BlockSpec((2, block_rows, col_tile), lambda c, d: (0, c, d))],
        out_specs=pl.BlockSpec(
            (replicas, 1, 1, 2 * row_tile, col_tile), lambda c, d: (0, c, d, 0, 0)
        ),
        out_shape=jax.ShapeDtypeStruct(
            (replicas, rows_split, cols_split, 2 * row_tile, col_tile), deltas.dtype
        ),
        compiler_params=pltpu.CompilerParams(vmem_limit_bytes=8 << 20),
    )(pltpu.with_memory_space_constraint(deltas, pltpu.HBM))


def mean_kernel(replicas, blocks, row_tile, col_tile, x_ref, mean_ref, shared_ref, squares_ref):
    lane_tiles = col_tile // LANES
    squares_ref[...] = jnp.zeros_like(squares_ref)

    def block(ab, carry):
        for group in range(2 * row_tile // 8):
            total = x_ref[0, ab, group * 8 : group * 8 + 8, :].astype(jnp.float32)
            for replica in range(1, replicas):
                total = total + x_ref[
                    replica, ab, group * 8 : group * 8 + 8, :
                ].astype(jnp.float32)
            mean = total * (1.0 / replicas)
            square = mean * mean
            partial = square[:, :LANES]
            for j in range(1, lane_tiles):
                partial = partial + square[:, j * LANES : (j + 1) * LANES]
            squares_ref[...] += partial
            row = 0
            while row < 8:
                at = group * 8 + row
                m, i = at // row_tile, at % row_tile
                count = min(8 - row, row_tile - i)
                start = ((m * blocks + ab) * row_tile + i) * lane_tiles
                for j in range(lane_tiles):
                    mean_ref[pl.ds(start + j, count, stride=lane_tiles), :] = mean[
                        row : row + count, j * LANES : (j + 1) * LANES
                    ]
                row += count
        return carry

    lax.fori_loop(0, blocks, block, 0)
    shared_ref[...] = jnp.broadcast_to(
        jnp.sum(squares_ref[...], axis=0, keepdims=True), shared_ref.shape
    )


def average(received, devices, row_tile, col_tile):
    replicas, blocks = received.shape[:2]
    size = blocks * 2 * row_tile * col_tile
    return pl.pallas_call(
        lambda *refs: mean_kernel(replicas, blocks, row_tile, col_tile, *refs),
        name="average",
        in_specs=[pl.BlockSpec(memory_space=pltpu.VMEM)],
        out_specs=[pl.BlockSpec(memory_space=pltpu.VMEM)] * 2,
        out_shape=[
            jax.ShapeDtypeStruct((size // LANES, LANES), jnp.float32),
            jax.ShapeDtypeStruct((devices, LANES), jnp.float32),
        ],
        scratch_shapes=[pltpu.VMEM((8, LANES), jnp.float32)],
        compiler_params=pltpu.CompilerParams(vmem_limit_bytes=4 << 20),
    )(received)


def step_kernel(entries, pieces, squares_ref, mean_ref, params_ref, momentum_ref, params_out, momentum_out, params_new, momentum_new, sems):
    squares = jnp.sum(squares_ref[...], keepdims=True)
    root_mean = jnp.sqrt(squares * (1.0 / entries) + epsilon)
    clip_scale = jnp.minimum(1.0, clip_level / root_mean)
    rows = mean_ref.shape[0] // pieces
    copies = []
    for piece in range(pieces):
        at = pl.ds(piece * rows, rows)
        gradient = clip_scale * mean_ref[at, :]
        momentum = moment_decay * momentum_ref[at, :] + gradient
        momentum_new[at, :] = momentum
        params_new[at, :] = params_ref[at, :] - outer_rate * (gradient + moment_decay * momentum)
        for n, (new, out) in enumerate(((momentum_new, momentum_out), (params_new, params_out))):
            copy = pltpu.make_async_copy(new.at[at], out.at[at], sems.at[n, piece])
            copy.start()
            copies.append(copy)
    for copy in copies:
        copy.wait()


def step(squares, mean, params, momentum, entries):
    pieces = 8
    return pl.pallas_call(
        lambda *refs: step_kernel(entries, pieces, *refs),
        name="outer_step",
        in_specs=[pl.BlockSpec(memory_space=pltpu.VMEM)] * 4,
        out_specs=[pl.BlockSpec(memory_space=pltpu.HBM)] * 2,
        out_shape=[jax.ShapeDtypeStruct(mean.shape, jnp.float32)] * 2,
        scratch_shapes=[
            pltpu.VMEM(mean.shape, jnp.float32),
            pltpu.VMEM(mean.shape, jnp.float32),
            pltpu.SemaphoreType.DMA((2, pieces)),
        ],
        compiler_params=pltpu.CompilerParams(vmem_limit_bytes=12 << 20),
    )(squares, mean, params, momentum)


def per_device(deltas, params, momentum):
    rows_split = lax.axis_size(GX)
    cols_split = lax.axis_size("gy")
    replicas = lax.axis_size(REP)
    devices = rows_split * cols_split * replicas
    matrices, local_rows, local_cols = deltas.shape[1:]
    row_tile = local_rows // (rows_split * replicas)
    col_tile = local_cols // cols_split
    entries = matrices * local_rows * local_cols * rows_split * cols_split
    packed = pack(deltas[0], replicas, rows_split, cols_split, row_tile, col_tile)
    packed = packed.reshape(devices, 2 * row_tile, col_tile)
    received = lax.all_to_all(packed, EVERY, split_axis=0, concat_axis=0, tiled=True)
    received = received.reshape(replicas, rows_split * cols_split, 2 * row_tile, col_tile)
    mean, squares = average(received, devices, row_tile, col_tile)
    squares = squares.reshape(devices, 1, LANES)
    squares = lax.all_to_all(squares, EVERY, split_axis=0, concat_axis=0, tiled=True)
    flat = mean.shape
    new_params, new_momentum = step(
        squares.reshape(devices, LANES), mean, params.reshape(flat), momentum.reshape(flat), entries
    )
    return new_params.reshape(params.shape), new_momentum.reshape(params.shape)


def solution(mesh):
    finer = Mesh(
        mesh.devices.reshape(2, 4, 2, 2, mesh.shape["gy"]), ("rep_0", "rep_1", "gx_0", "gx_1", "gy")
    )
    return jax.shard_map(
        per_device,
        mesh=finer,
        in_specs=(
            P(REP, None, GX, "gy"),
            P(None, None, GX, REP, None, "gy", None, None),
            P(None, None, GX, REP, None, "gy", None, None),
        ),
        out_specs=(
            P(None, None, GX, REP, None, "gy", None, None),
            P(None, None, GX, REP, None, "gy", None, None),
        ),
        check_vma=False,
    )
```

```python
import jax
import jax.numpy as jnp
from jax import lax
from jax.experimental import pallas as pl
from jax.experimental.pallas import tpu as pltpu
from jax.sharding import Mesh
from jax.sharding import PartitionSpec as P

GX = ("gx_0", "gx_1")
REP = ("rep_0", "rep_1")
EVERY = ("gy", "rep_1", "rep_0", "gx_0", "gx_1")
LANES = 128

clip_level = 0.25
moment_decay = 0.9
outer_rate = 0.7
epsilon = 1e-06


def pack_kernel(row_tile, x_ref, out_ref, landed, sems):
    cols_split, inner, outer, rows_split = out_ref.shape[:4]
    col_tile = out_ref.shape[5]
    block_rows = outer * inner * row_tile
    copies = {}
    for c in range(rows_split):
        for m in range(2):
            at = pl.ds(c * block_rows, block_rows)
            copies[c, m] = pltpu.make_async_copy(
                x_ref.at[m, at, :], landed.at[m, at, :], sems.at[c, m]
            )
            copies[c, m].start()
    for c in range(rows_split):
        for m in range(2):
            copies[c, m].wait()
            for r in range(outer * inner):
                row = c * block_rows + r * row_tile
                for d in range(cols_split):
                    out_ref[d, r % inner, r // inner, c, m * row_tile : (m + 1) * row_tile, :] = (
                        landed[m, row : row + row_tile, d * col_tile : (d + 1) * col_tile]
                    )


def pack(deltas, slots, row_tile, col_tile):
    return pl.pallas_call(
        lambda *refs: pack_kernel(row_tile, *refs),
        name="pack",
        in_specs=[pl.BlockSpec(memory_space=pltpu.HBM)],
        out_specs=pl.BlockSpec(memory_space=pltpu.VMEM),
        out_shape=jax.ShapeDtypeStruct((*slots, 2 * row_tile, col_tile), deltas.dtype),
        scratch_shapes=[
            pltpu.VMEM(deltas.shape, deltas.dtype),
            pltpu.SemaphoreType.DMA((slots[3], 2)),
        ],
        compiler_params=pltpu.CompilerParams(vmem_limit_bytes=16 << 20),
    )(pltpu.with_memory_space_constraint(deltas, pltpu.HBM))


def mean_kernel(x_ref, mean_ref, shared_ref, squares_ref):
    cols_split, inner, outer, rows_split, rows, columns = x_ref.shape
    row_tile, lane_tiles = rows // 2, columns // LANES
    blocks = rows_split * cols_split
    squares_ref[...] = jnp.zeros_like(squares_ref)

    def block(ab, carry):
        a, b = ab // cols_split, ab % cols_split
        for group in range(rows // 8):
            at = slice(group * 8, group * 8 + 8)
            total = x_ref[b, 0, 0, a, at, :].astype(jnp.float32)
            for r in range(1, outer * inner):
                total = total + x_ref[b, r % inner, r // inner, a, at, :].astype(jnp.float32)
            mean = total * (1.0 / (outer * inner))
            square = mean * mean
            partial = square[:, :LANES]
            for j in range(1, lane_tiles):
                partial = partial + square[:, j * LANES : (j + 1) * LANES]
            squares_ref[...] += partial
            row = 0
            while row < 8:
                m, i = (group * 8 + row) // row_tile, (group * 8 + row) % row_tile
                count = min(8 - row, row_tile - i)
                start = ((m * blocks + ab) * row_tile + i) * lane_tiles
                for j in range(lane_tiles):
                    mean_ref[pl.ds(start + j, count, stride=lane_tiles), :] = mean[
                        row : row + count, j * LANES : (j + 1) * LANES
                    ]
                row += count
        return carry

    lax.fori_loop(0, blocks, block, 0)
    shared_ref[...] = jnp.broadcast_to(
        jnp.sum(squares_ref[...], axis=0, keepdims=True), shared_ref.shape
    )


def average(received, devices):
    cols_split, _, _, rows_split, rows, columns = received.shape
    return pl.pallas_call(
        mean_kernel,
        name="average",
        in_specs=[pl.BlockSpec(memory_space=pltpu.VMEM)],
        out_specs=[pl.BlockSpec(memory_space=pltpu.VMEM)] * 2,
        out_shape=[
            jax.ShapeDtypeStruct(
                (cols_split * rows_split * rows * columns // LANES, LANES), jnp.float32
            ),
            jax.ShapeDtypeStruct((devices, LANES), jnp.float32),
        ],
        scratch_shapes=[pltpu.VMEM((8, LANES), jnp.float32)],
        compiler_params=pltpu.CompilerParams(vmem_limit_bytes=4 << 20),
    )(received)


def step_kernel(entries, pieces, squares_ref, mean_ref, params_ref, momentum_ref, params_out, momentum_out, params_new, momentum_new, sems):
    squares = jnp.sum(squares_ref[...], keepdims=True)
    root_mean = jnp.sqrt(squares * (1.0 / entries) + epsilon)
    clip_scale = jnp.minimum(1.0, clip_level / root_mean)
    rows = mean_ref.shape[0] // pieces
    copies = []
    for piece in range(pieces):
        at = pl.ds(piece * rows, rows)
        gradient = clip_scale * mean_ref[at, :]
        momentum = moment_decay * momentum_ref[at, :] + gradient
        momentum_new[at, :] = momentum
        params_new[at, :] = params_ref[at, :] - outer_rate * (gradient + moment_decay * momentum)
        for n, (new, out) in enumerate(((momentum_new, momentum_out), (params_new, params_out))):
            copy = pltpu.make_async_copy(new.at[at], out.at[at], sems.at[n, piece])
            copy.start()
            copies.append(copy)
    for copy in copies:
        copy.wait()


def step(squares, mean, params, momentum, entries):
    pieces = 8
    return pl.pallas_call(
        lambda *refs: step_kernel(entries, pieces, *refs),
        name="outer_step",
        in_specs=[pl.BlockSpec(memory_space=pltpu.VMEM)] * 4,
        out_specs=[pl.BlockSpec(memory_space=pltpu.HBM)] * 2,
        out_shape=[jax.ShapeDtypeStruct(mean.shape, jnp.float32)] * 2,
        scratch_shapes=[
            pltpu.VMEM(mean.shape, jnp.float32),
            pltpu.VMEM(mean.shape, jnp.float32),
            pltpu.SemaphoreType.DMA((2, pieces)),
        ],
        compiler_params=pltpu.CompilerParams(vmem_limit_bytes=12 << 20),
    )(squares, mean, params, momentum)


def per_device(deltas, params, momentum):
    rows_split = lax.axis_size(GX)
    cols_split = lax.axis_size("gy")
    replicas = lax.axis_size(REP)
    devices = rows_split * cols_split * replicas
    matrices, local_rows, local_cols = deltas.shape[1:]
    row_tile = local_rows // (rows_split * replicas)
    col_tile = local_cols // cols_split
    entries = matrices * local_rows * local_cols * rows_split * cols_split
    slots = (cols_split, *(lax.axis_size(n) for n in reversed(REP)), rows_split)
    packed = pack(deltas[0], slots, row_tile, col_tile)
    received = lax.all_to_all(
        packed.reshape(devices, 2 * row_tile, col_tile),
        EVERY,
        split_axis=0,
        concat_axis=0,
        tiled=True,
    )
    mean, squares = average(received.reshape(packed.shape), devices)
    squares = squares.reshape(devices, 1, LANES)
    squares = lax.all_to_all(squares, EVERY, split_axis=0, concat_axis=0, tiled=True)
    flat = mean.shape
    new_params, new_momentum = step(
        squares.reshape(devices, LANES), mean, params.reshape(flat), momentum.reshape(flat), entries
    )
    return new_params.reshape(params.shape), new_momentum.reshape(params.shape)


def solution(mesh):
    finer = Mesh(
        mesh.devices.reshape(2, 4, 2, 2, mesh.shape["gy"]), ("rep_0", "rep_1", "gx_0", "gx_1", "gy")
    )
    return jax.shard_map(
        per_device,
        mesh=finer,
        in_specs=(
            P(REP, None, GX, "gy"),
            P(None, None, GX, REP, None, "gy", None, None),
            P(None, None, GX, REP, None, "gy", None, None),
        ),
        out_specs=(
            P(None, None, GX, REP, None, "gy", None, None),
            P(None, None, GX, REP, None, "gy", None, None),
        ),
        check_vma=False,
    )
```

```python
import jax
import jax.numpy as jnp
from jax import lax
from jax.experimental import pallas as pl
from jax.experimental.pallas import tpu as pltpu
from jax.sharding import Mesh
from jax.sharding import PartitionSpec as P

GX = ("gx_0", "gx_1")
REP = ("rep_0", "rep_1")
EVERY = ("gy", "rep_1", "rep_0", "gx_0", "gx_1")
LANES = 128

clip_level = 0.25
moment_decay = 0.9
outer_rate = 0.7
epsilon = 1e-06


def pack_kernel(row_tile, x_ref, out_ref, landed, sems):
    cols_split, inner, outer, rows_split = out_ref.shape[:4]
    col_tile = out_ref.shape[5]
    block_rows = outer * inner * row_tile
    copies = {}
    for c in range(rows_split):
        for m in range(2):
            at = pl.ds(c * block_rows, block_rows)
            copies[c, m] = pltpu.make_async_copy(
                x_ref.at[m, at, :], landed.at[m, at, :], sems.at[c, m]
            )
            copies[c, m].start()
    for c in range(rows_split):
        for m in range(2):
            copies[c, m].wait()
            for r in range(outer * inner):
                row = c * block_rows + r * row_tile
                for d in range(cols_split):
                    out_ref[d, r % inner, r // inner, c, m * row_tile : (m + 1) * row_tile, :] = (
                        landed[m, row : row + row_tile, d * col_tile : (d + 1) * col_tile]
                    )


def pack(deltas, slots, row_tile, col_tile):
    return pl.pallas_call(
        lambda *refs: pack_kernel(row_tile, *refs),
        name="pack",
        in_specs=[pl.BlockSpec(memory_space=pltpu.HBM)],
        out_specs=pl.BlockSpec(memory_space=pltpu.VMEM),
        out_shape=jax.ShapeDtypeStruct((*slots, 2 * row_tile, col_tile), deltas.dtype),
        scratch_shapes=[
            pltpu.VMEM(deltas.shape, deltas.dtype),
            pltpu.SemaphoreType.DMA((slots[3], 2)),
        ],
        compiler_params=pltpu.CompilerParams(vmem_limit_bytes=16 << 20),
    )(pltpu.with_memory_space_constraint(deltas, pltpu.HBM))


def sum_kernel(x_ref, sum_ref, shared_ref):
    cols_split, inner, outer, rows_split, rows, columns = x_ref.shape
    row_tile, lane_tiles = rows // 2, columns // LANES
    blocks = rows_split * cols_split

    def block(ab, squares):
        a, b = ab // cols_split, ab % cols_split
        for group in range(rows // 8):
            at = slice(group * 8, group * 8 + 8)
            total = x_ref[b, 0, 0, a, at, :].astype(jnp.float32)
            for r in range(1, outer * inner):
                total = total + x_ref[b, r % inner, r // inner, a, at, :].astype(jnp.float32)
            square = total * total
            partial = square[:, :LANES]
            for j in range(1, lane_tiles):
                partial = partial + square[:, j * LANES : (j + 1) * LANES]
            squares = squares + partial
            row = 0
            while row < 8:
                m, i = (group * 8 + row) // row_tile, (group * 8 + row) % row_tile
                count = min(8 - row, row_tile - i)
                start = ((m * blocks + ab) * row_tile + i) * lane_tiles
                for j in range(lane_tiles):
                    sum_ref[pl.ds(start + j, count, stride=lane_tiles), :] = total[
                        row : row + count, j * LANES : (j + 1) * LANES
                    ]
                row += count
        return squares

    squares = lax.fori_loop(0, blocks, block, jnp.zeros((8, LANES), jnp.float32))
    shared_ref[...] = jnp.broadcast_to(
        jnp.sum(squares, axis=0, keepdims=True), shared_ref.shape
    )


def add_up(received, devices):
    cols_split, _, _, rows_split, rows, columns = received.shape
    return pl.pallas_call(
        sum_kernel,
        name="add_up",
        in_specs=[pl.BlockSpec(memory_space=pltpu.VMEM)],
        out_specs=[pl.BlockSpec(memory_space=pltpu.VMEM)] * 2,
        out_shape=[
            jax.ShapeDtypeStruct(
                (cols_split * rows_split * rows * columns // LANES, LANES), jnp.float32
            ),
            jax.ShapeDtypeStruct((devices, LANES), jnp.float32),
        ],
        compiler_params=pltpu.CompilerParams(vmem_limit_bytes=4 << 20),
    )(received)


def step_kernel(entries, replicas, cuts, squares_ref, sum_ref, params_ref, momentum_ref, params_out, momentum_out, params_new, momentum_new, sems):
    squares = jnp.sum(squares_ref[...], keepdims=True) * (1.0 / replicas**2)
    root_mean = jnp.sqrt(squares * (1.0 / entries) + epsilon)
    sum_scale = jnp.minimum(1.0, clip_level / root_mean) * (1.0 / replicas)
    copies = []
    for piece, (low, high) in enumerate(zip(cuts, cuts[1:])):
        at = pl.ds(low, high - low)
        gradient = sum_scale * sum_ref[at, :]
        momentum = moment_decay * momentum_ref[at, :] + gradient
        momentum_new[at, :] = momentum
        params_new[at, :] = params_ref[at, :] - outer_rate * (gradient + moment_decay * momentum)
        for n, (new, out) in enumerate(((momentum_new, momentum_out), (params_new, params_out))):
            copy = pltpu.make_async_copy(new.at[at], out.at[at], sems.at[n, piece])
            copy.start()
            copies.append(copy)
    for copy in copies:
        copy.wait()


def step(squares, total, params, momentum, entries, replicas):
    tiles = total.shape[0] // 8
    shares = (1, 2, 4, 4, 4, 4, 4, 4, 1)
    cuts = [tiles * sum(shares[:n]) // sum(shares) * 8 for n in range(len(shares) + 1)]
    return pl.pallas_call(
        lambda *refs: step_kernel(entries, replicas, cuts, *refs),
        name="outer_step",
        in_specs=[pl.BlockSpec(memory_space=pltpu.VMEM)] * 4,
        out_specs=[pl.BlockSpec(memory_space=pltpu.HBM)] * 2,
        out_shape=[jax.ShapeDtypeStruct(total.shape, jnp.float32)] * 2,
        scratch_shapes=[
            pltpu.VMEM(total.shape, jnp.float32),
            pltpu.VMEM(total.shape, jnp.float32),
            pltpu.SemaphoreType.DMA((2, len(shares))),
        ],
        compiler_params=pltpu.CompilerParams(vmem_limit_bytes=12 << 20),
    )(squares, total, params, momentum)


def per_device(deltas, params, momentum):
    rows_split = lax.axis_size(GX)
    cols_split = lax.axis_size("gy")
    replicas = lax.axis_size(REP)
    devices = rows_split * cols_split * replicas
    matrices, local_rows, local_cols = deltas.shape[1:]
    row_tile = local_rows // (rows_split * replicas)
    col_tile = local_cols // cols_split
    entries = matrices * local_rows * local_cols * rows_split * cols_split
    slots = (cols_split, *(lax.axis_size(n) for n in reversed(REP)), rows_split)
    packed = pack(deltas[0], slots, row_tile, col_tile)
    received = lax.all_to_all(
        packed.reshape(devices, 2 * row_tile, col_tile),
        EVERY,
        split_axis=0,
        concat_axis=0,
        tiled=True,
    )
    total, squares = add_up(received.reshape(packed.shape), devices)
    squares = squares.reshape(devices, 1, LANES)
    squares = lax.all_to_all(squares, EVERY, split_axis=0, concat_axis=0, tiled=True)
    flat = total.shape
    new_params, new_momentum = step(
        squares.reshape(devices, LANES), total, params.reshape(flat), momentum.reshape(flat), entries, replicas
    )
    return new_params.reshape(params.shape), new_momentum.reshape(params.shape)


def solution(mesh):
    finer = Mesh(
        mesh.devices.reshape(2, 4, 2, 2, mesh.shape["gy"]), ("rep_0", "rep_1", "gx_0", "gx_1", "gy")
    )
    return jax.shard_map(
        per_device,
        mesh=finer,
        in_specs=(
            P(REP, None, GX, "gy"),
            P(None, None, GX, REP, None, "gy", None, None),
            P(None, None, GX, REP, None, "gy", None, None),
        ),
        out_specs=(
            P(None, None, GX, REP, None, "gy", None, None),
            P(None, None, GX, REP, None, "gy", None, None),
        ),
        check_vma=False,
    )
```
